512 devices in a mesh: orb: 32 (over y_hi, x, core), grp: 16 (over y_lo, z).
Axes of the slice: x: 4, y: 8 (y_hi: 4, y_lo: 2; y = y_hi * 2 + y_lo), z: 8, core: 2. Of those that a mesh axis runs over, the one named last changes fastest.
Arguments:
- orbitals: bfloat16 [512, 64000], P(('orb', 'grp')), may hold values from -8 to 8
Outputs:
- projector: bfloat16 [512, 64000], P(('orb', 'grp'))
The draws below stay inside these ranges and needn't reach their ends.
All inputs are finite; a program needn't handle non-finite values.
Results may differ from the reference program's by a relative error of at most 0.0012.
The reference program's roundings to bfloat16 on the way (of `exchange` and `inverse`) count: a program that leaves them out, or rounds other values in their place, can miss the bound.
Values may be sent and summed in bfloat16 or wider, within the bound.
No kernel may reach another device: no remote copies, remote signals or barrier semaphores. Data moves between devices by JAX's collectives and lax.ppermute only.
A program may use at most 64 MiB of HBM per device.

```python
import math
import jax
import jax.numpy as jnp
from jax import lax

GRID = 40
STEPS = 3
CELLS = 64000
N = 512
N_ORB = 32
N_GRP = 16


def draw_orbitals(key, part):
    noise_key = jax.random.fold_in(key, 11)
    scale_key = jax.random.fold_in(key, 23)
    field_key = jax.random.fold_in(key, 37)
    plane = (jnp.arange(CELLS, dtype=jnp.int32) // (GRID * GRID)).astype(jnp.float32)
    envelope = jnp.exp(0.5 * math.log(3.0) * plane / (GRID - 1))
    noise = jax.random.normal(noise_key, (N, CELLS), jnp.float32)
    shared = jax.random.normal(field_key, (1, CELLS), jnp.float32)
    mixed = 0.7 * shared + 0.7 * noise
    scales = jnp.exp(jax.random.uniform(scale_key, (N, 1), jnp.float32, math.log(0.7), math.log(1.4)))
    values = jnp.clip(mixed * scales * envelope[None, :], -8.0, 8.0)
    return values.astype(jnp.bfloat16)


def setup_inputs(seed: int = 0) -> dict:
    splits = jax.random.split(jax.random.key(seed), 2)
    orbitals = draw_orbitals(jax.random.fold_in(splits[1], 71), 0)
    return {"orbitals": orbitals}


def kernel_table(size):
    freq = jnp.arange(size, dtype=jnp.int32)
    signed = jnp.where(freq <= size // 2, freq, freq - size).astype(jnp.float32)
    wave = 2.0 * math.pi / size * signed
    square = wave * wave
    total = square[:, None, None] + square[None, :, None] + square[None, None, :]
    safe = jnp.where(total > 0, total, 1.0)
    return jnp.where(total > 0, 4.0 * (1.0 - jnp.exp(-0.25 * total)) / safe, 1.0)

def pair_terms(pair, kernel):
    target, source = pair
    density = target.astype(jnp.float32) * source.astype(jnp.float32)
    volume = density.reshape(-1, GRID, GRID, GRID)
    spectrum = jnp.fft.fftn(volume, axes=(1, 2, 3)) * kernel
    potential = jnp.real(jnp.fft.ifftn(spectrum, axes=(1, 2, 3))).astype(jnp.float32)
    return source.astype(jnp.float32) * potential.reshape(density.shape)

def factorize(margin):
    symmetric = 0.5 * (margin + margin.T)
    magnitude = jnp.abs(symmetric)
    gamma = jnp.mean(jnp.diagonal(magnitude)) + 1e-06
    regularized = jnp.diag(jnp.sum(magnitude, axis=1) + gamma) - symmetric
    factor = jnp.linalg.cholesky(regularized)
    identity = jnp.eye(symmetric.shape[0], dtype=jnp.float32)
    inverse = jax.scipy.linalg.solve_triangular(factor, identity, lower=True)
    return inverse.astype(jnp.bfloat16)

def reference(orbitals):
    kernel = kernel_table(GRID)
    blocks = orbitals.reshape(N_ORB, N_GRP, CELLS)
    exchange = jnp.zeros((N, CELLS), jnp.float32)
    for step in range(STEPS):
        sources = jnp.roll(blocks, step, axis=0)
        terms = lax.map(lambda pair: pair_terms(pair, kernel), (blocks, sources))
        exchange = exchange - terms.reshape(N, CELLS)
    compact = exchange.astype(jnp.bfloat16)
    margin = jnp.dot(orbitals.astype(jnp.float32), compact.T.astype(jnp.float32), preferred_element_type=jnp.float32) / CELLS
    inverse = factorize(margin)
    return jnp.dot(inverse.astype(jnp.float32), compact.astype(jnp.float32), preferred_element_type=jnp.float32).astype(jnp.bfloat16)
```

```python
import math
import numpy as np
import jax
import jax.numpy as jnp
from jax import lax
from jax.experimental import pallas as pl
from jax.experimental.pallas import tpu as pltpu
from jax.sharding import Mesh
from jax.sharding import PartitionSpec as P


GRID = 40
CELLS = GRID**3
F32 = jnp.float32
BF16 = jnp.bfloat16


def cosine_sums(values, size):
    half = size // 2
    out = [None] * (half + 1)
    if size % 4 == 0:
        mid = half // 2
        folded = [values[x] + values[half - x] for x in range(mid)] + [values[mid]]
        for b, term in enumerate(cosine_sums(folded, half)):
            out[2 * b] = term
        rest = [values[x] - values[half - x] for x in range(mid)]
        for a in range(1, half + 1, 2):
            out[a] = weighted(rest, [math.cos(2 * math.pi * (a * x % size) / size) for x in range(mid)])
    else:
        for a in range(half + 1):
            out[a] = weighted(values, [math.cos(2 * math.pi * (a * x % size) / size) for x in range(half + 1)])
    return out


def sine_sums(values, size):
    half = size // 2
    out = [None] * (half + 1)
    if size % 4 == 0:
        mid = half // 2
        folded = [None] + [values[x] - values[half - x] for x in range(1, mid)]
        for b, term in enumerate(sine_sums(folded, half)):
            if term is not None:
                out[2 * b] = term
        rest = [values[x] + values[half - x] for x in range(1, mid)] + [values[mid]]
        for a in range(1, half, 2):
            out[a] = weighted(rest, [math.sin(2 * math.pi * (a * x % size) / size) for x in range(1, mid + 1)])
    else:
        for a in range(1, half):
            out[a] = weighted(values[1:half], [math.sin(2 * math.pi * (a * x % size) / size) for x in range(1, half)])
    return out


def weighted(values, weights):
    groups = {}
    for value, weight in zip(values, weights, strict=True):
        size = round(abs(weight), 12)
        if size == 0.0:
            continue
        groups.setdefault(size, []).append(value if weight > 0 else (value,))
    total = None
    for size, members in groups.items():
        part = None
        for m in members:
            if isinstance(m, tuple):
                part = -m[0] if part is None else part - m[0]
            else:
                part = m if part is None else part + m
        part = part if size == 1.0 else part * size
        total = part if total is None else total + part
    return total


def hartley(values):
    size = len(values)
    half = size // 2
    even = [values[0]] + [values[x] + values[size - x] for x in range(1, half)] + [values[half]]
    odd = [None] + [values[x] - values[size - x] for x in range(1, half)]
    cosines, sines = cosine_sums(even, size), sine_sums(odd, size)
    out = [None] * size
    out[0], out[half] = cosines[0], cosines[half]
    for a in range(1, half):
        out[a] = cosines[a] + sines[a]
        out[size - a] = cosines[a] - sines[a]
    return out


def split(x):
    high = x.astype(BF16)
    return high, (x - high.astype(F32)).astype(BF16)


def along_lanes(x, table_high, table_low):
    high, low = split(x)
    out = jnp.dot(high, table_high, preferred_element_type=F32)
    out += jnp.dot(low, table_high, preferred_element_type=F32)
    return out + jnp.dot(high, table_low, preferred_element_type=F32)


ROWS = 200


def exchange_kernel(o_ref, a_ref, b_ref, table_ref, kernel_ref, out_ref, field, sources):
    high, low = table_ref[0], table_ref[1]

    @pl.loop(0, GRID * GRID // ROWS)
    def _(step):
        rows = pl.ds(pl.multiple_of(step * ROWS, 8), ROWS)
        o = o_ref[rows, :].astype(F32)
        three = jnp.concatenate(
            [o, a_ref[rows, :].astype(F32), b_ref[rows, :].astype(F32), jnp.zeros((ROWS, 8), F32)], axis=1
        )
        target = jnp.concatenate([o, o, o, jnp.zeros((ROWS, 8), F32)], axis=1)
        sources[rows, :] = three
        field[rows, :] = along_lanes(target * three, high, low)

    @pl.loop(0, GRID // 8)
    def _(chunk):
        rows = [pl.ds(pl.multiple_of(GRID * x + 8 * chunk, 8), 8) for x in range(GRID)]
        for x, value in enumerate(hartley([field[r, :] for r in rows])):
            field[rows[x], :] = value

    @pl.loop(0, GRID // 8)
    def _(chunk):
        rows = [pl.ds(y + GRID * 8 * chunk, 8, stride=GRID) for y in range(GRID)]
        spectrum = hartley([field[r, :] for r in rows])
        around = pl.ds(pl.multiple_of(8 * chunk, 8), 8)
        spectrum = [v * kernel_ref[min(b, GRID - b), around, :] for b, v in enumerate(spectrum)]
        for y, value in enumerate(hartley(spectrum)):
            field[rows[y], :] = value

    @pl.loop(0, GRID // 8)
    def _(chunk):
        rows = [pl.ds(pl.multiple_of(GRID * x + 8 * chunk, 8), 8) for x in range(GRID)]
        for x, value in enumerate(hartley([field[r, :] for r in rows])):
            field[rows[x], :] = value

    @pl.loop(0, GRID * GRID // ROWS)
    def _(step):
        rows = pl.ds(pl.multiple_of(step * ROWS, 8), ROWS)
        terms = sources[rows, :] * along_lanes(field[rows, :], high, low)
        total = terms + pltpu.roll(terms, 128 - GRID, axis=1) + pltpu.roll(terms, 128 - 2 * GRID, axis=1)
        out_ref[rows, :] = (-total[:, :GRID]).astype(BF16)


def hartley_tables():
    index = np.arange(GRID)
    angle = 2 * np.pi / GRID * (index[:, None] * index[None, :] % GRID)
    cas = (np.cos(angle) + np.sin(angle)).astype(np.float32)
    table = np.zeros((128, 128), np.float32)
    for s in range(3):
        table[GRID * s : GRID * (s + 1), GRID * s : GRID * (s + 1)] = cas
    high = jnp.asarray(table).astype(BF16)
    low = (jnp.asarray(table) - high.astype(F32)).astype(BF16)
    return jnp.stack([high, low])


def kernel_table():
    freq = np.arange(GRID)
    wave = 2 * np.pi / GRID * np.where(freq <= GRID // 2, freq, freq - GRID)
    square = wave * wave
    total = square[: GRID // 2 + 1, None, None] + square[None, :, None] + square[None, None, :]
    safe = np.where(total > 0, total, 1.0)
    table = np.where(total > 0, 4 * (1 - np.exp(-0.25 * total)) / safe, 1.0) / CELLS
    out = np.zeros((GRID // 2 + 1, GRID, 128), np.float32)
    for s in range(3):
        out[:, :, GRID * s : GRID * (s + 1)] = table
    return jnp.asarray(out)


def exchange_of(o, a, b):
    square = GRID * GRID
    return pl.pallas_call(
        exchange_kernel,
        out_shape=jax.ShapeDtypeStruct((square, GRID), BF16),
        in_specs=[pl.BlockSpec(memory_space=pltpu.VMEM)] * 5,
        out_specs=pl.BlockSpec(memory_space=pltpu.VMEM),
        scratch_shapes=[pltpu.VMEM((square, 128), F32), pltpu.VMEM((square, 128), F32)],
        compiler_params=pltpu.CompilerParams(vmem_limit_bytes=32 << 20),
        cost_estimate=pl.CostEstimate(flops=10_000_000, bytes_accessed=4_000_000, transcendentals=0),
        name="exchange",
    )(o.reshape(square, GRID), a.reshape(square, GRID), b.reshape(square, GRID), hartley_tables(), kernel_table())


N = 512
BLOCK = 128


def thirds(x):
    high = x.astype(BF16)
    rest = x - high.astype(F32)
    middle = rest.astype(BF16)
    return high, middle, (rest - middle.astype(F32)).astype(BF16)


def exact_dot(a, b):
    (a0, a1, a2), (b0, b1, b2) = thirds(a), thirds(b)
    d = lambda p, q: jnp.dot(p, q, preferred_element_type=F32)
    return d(a0, b0) + (d(a0, b1) + d(a1, b0)) + (d(a1, b1) + d(a0, b2) + d(a2, b0))


def invert_block(groups):
    sub = lax.broadcasted_iota(jnp.int32, (8, BLOCK), 0)
    lane = lax.broadcasted_iota(jnp.int32, (8, BLOCK), 1)
    wide = lambda x, j: jnp.broadcast_to(x[j : j + 1, :], (8, BLOCK))
    for p in range(BLOCK // 8):
        here = (lane >= 8 * p) & (lane < 8 * p + 8)
        column = lambda v, k: jnp.broadcast_to(groups[v][:, 8 * p + k : 8 * p + k + 1], (8, BLOCK))
        pivots = [column(p, k) for k in range(8)]
        below = {v: [column(v, k) for k in range(8)] for v in range(p + 1, BLOCK // 8)}
        panel = jnp.where(here, jnp.where(lane - 8 * p == sub, 1.0, 0.0), groups[p])
        lower = jnp.zeros((8, BLOCK), F32)
        scale = jnp.zeros((8, BLOCK), F32)
        for j in range(8):
            r = 1.0 / wide(pivots[j], j)
            factor = jnp.where(sub == j, 0.0, pivots[j])
            row = wide(panel, j)
            lower = jnp.where(sub == j, row, lower)
            scale = jnp.where(sub == j, r, scale)
            for k in range(j + 1, 8):
                pivots[k] = pivots[k] - (factor * wide(pivots[k], j)) * r
            panel = panel - (factor * row) * r
        panel = panel * scale
        groups[p] = lower * jnp.sqrt(scale)
        spread = [wide(panel, k) for k in range(8)]
        for v in range(p + 1, BLOCK // 8):
            value = jnp.where(here, 0.0, groups[v])
            for k in range(8):
                value = value - below[v][k] * spread[k]
            groups[v] = value
    return groups


def factor_kernel(place_ref, parts_ref, out_ref, m, w):
    core, column, block = place_ref[0], place_ref[1], place_ref[2]
    for r in range(4):
        for q in range(4):
            for p in range(4):
                top = BLOCK * p + 32 * q
                part = parts_ref[(p // 2) ^ core, 4 * r + q, 32 * (p % 2) : 32 * (p % 2) + 32, :]
                m[top : top + 32, BLOCK * r : BLOCK * (r + 1)] = part
    rows = lambda i: slice(BLOCK * i, BLOCK * (i + 1))
    eye = lax.broadcasted_iota(jnp.int32, (BLOCK, BLOCK), 0) == lax.broadcasted_iota(jnp.int32, (BLOCK, BLOCK), 1)
    sums = [jnp.zeros((1, BLOCK), F32) for _ in range(4)]
    trace = jnp.zeros((1, BLOCK), F32)
    for i in range(4):
        for j in range(i + 1):
            s = (m[rows(i), rows(j)] + m[rows(j), rows(i)].T) * (-0.5 / CELLS)
            flipped = s.T
            m[rows(i), rows(j)] = s
            sums[j] = sums[j] + jnp.sum(jnp.abs(s), axis=0, keepdims=True)
            if i != j:
                m[rows(j), rows(i)] = flipped
                sums[i] = sums[i] + jnp.sum(jnp.abs(flipped), axis=0, keepdims=True)
            else:
                trace = trace + jnp.sum(jnp.where(eye, jnp.abs(s), 0.0), axis=0, keepdims=True)
    gamma = jnp.sum(trace, axis=1, keepdims=True) / N + 1e-6
    for i in range(4):
        m[rows(i), rows(i)] = m[rows(i), rows(i)] + jnp.where(eye, sums[i] + gamma, 0.0)

    @pl.loop(0, 4)
    def _(s):
        here = pl.ds(pl.multiple_of(s * BLOCK, BLOCK), BLOCK)
        groups = [m[pl.ds(pl.multiple_of(s * BLOCK + 8 * v, 8), 8), here] for v in range(BLOCK // 8)]
        for v, value in enumerate(invert_block(groups)):
            w[8 * v : 8 * v + 8, :] = value
        lower = lax.broadcasted_iota(jnp.int32, (BLOCK, BLOCK), 0) >= lax.broadcasted_iota(jnp.int32, (BLOCK, BLOCK), 1)
        inverse = jnp.where(lower, w[...], 0.0)
        m[here, :] = exact_dot(inverse, m[here, :])
        m[here, here] = inverse
        for i in range(1, 4):

            @pl.when(i > s)
            def _():
                left = m[here, rows(i)].T
                m[rows(i), here] = jnp.zeros((BLOCK, BLOCK), F32)
                m[rows(i), :] = m[rows(i), :] - exact_dot(left, m[here, :])

    mine = pl.ds(pl.multiple_of(32 * block, 32), 32)
    row = lax.broadcasted_iota(jnp.int32, (32, BLOCK), 0) + 32 * block
    lane = lax.broadcasted_iota(jnp.int32, (32, BLOCK), 1)
    values = [jnp.where(lane + BLOCK * p <= row, m[mine, BLOCK * p : BLOCK * (p + 1)], 0.0) for p in range(4)]
    for k in range(4):
        s = lax.rem(column + 4 - k, 4)
        total = jnp.zeros((32, BLOCK), F32)
        for p, value in enumerate(values):
            turned = pltpu.roll(value, lax.rem(p + 4 - s, 4) * 32, axis=1)
            total = jnp.where(lane // 32 == p, turned, total)
        out_ref[k] = total.astype(BF16)


def inverse_rows(place, parts):
    return pl.pallas_call(
        factor_kernel,
        out_shape=jax.ShapeDtypeStruct((4, 32, BLOCK), BF16),
        in_specs=[pl.BlockSpec(memory_space=pltpu.SMEM), pl.BlockSpec(memory_space=pltpu.VMEM)],
        out_specs=pl.BlockSpec(memory_space=pltpu.VMEM),
        scratch_shapes=[pltpu.VMEM((N, N), F32), pltpu.VMEM((BLOCK, BLOCK), F32)],
        compiler_params=pltpu.CompilerParams(vmem_limit_bytes=32 << 20),
        cost_estimate=pl.CostEstimate(flops=400_000_000, bytes_accessed=4_000_000, transcendentals=0),
        name="factor",
    )(place, parts)


AXES = ("yh", "x", "c", "yl", "z")
BLOCKS = ("yh", "x", "c")
SLABS = ("c", "yl", "z")
SHELF = ("yl", "z")
PLANE = ("yh", "x")


def shifted(value, axes, steps):
    count = lax.axis_size(axes)
    return lax.ppermute(value, axes, [(i, (i + steps) % count) for i in range(count)])


def swapped(tiles, axes):
    return lax.all_to_all(tiles, axes, split_axis=0, concat_axis=0, tiled=True)


def shown_to(value, axes):
    return swapped(jnp.broadcast_to(value, (lax.axis_size(axes), *value.shape)), axes)


def gathered_slab(row, axis):
    slabs, copies = lax.axis_size(SLABS), lax.axis_size(axis)
    tiles = jnp.broadcast_to(row.reshape(1, slabs, 2, -1), (copies, slabs, 2, CELLS // slabs // 2))
    return swapped(tiles.reshape(copies * slabs, 2, -1), (axis, *SLABS)).reshape(copies * slabs, -1)


def around(value, axes, way):
    pieces = [value]
    for k in range(1, lax.axis_size(axes)):
        pieces.append(shifted(value, axes, way * k))
    return pieces


def steps(orbitals):
    slabs = lax.axis_size(SLABS)
    width = CELLS // slabs
    first, second = shifted(orbitals, BLOCKS, 1), shifted(orbitals, BLOCKS, 2)
    orbital_rows = gathered_slab(orbitals, "x")
    exchange = exchange_of(orbitals, first, second)
    exchange_rows = gathered_slab(exchange, "yh")
    margin = lax.dot_general(
        exchange_rows, orbital_rows, (((1,), (1,)), ((), ())), preferred_element_type=F32
    )
    summed = jnp.sum(swapped(margin.reshape(slabs, BLOCK // slabs, BLOCK), SLABS), axis=0)
    half = shown_to(summed, SHELF).reshape(BLOCK // 2, BLOCK)
    mine = shown_to(half, PLANE)
    other = shifted(mine, ("c",), 1)
    place = jnp.stack([lax.axis_index("c"), lax.axis_index("x"), lax.axis_index(PLANE)]).astype(jnp.int32)
    rows = inverse_rows(place, jnp.stack([mine, other]))
    projected = jnp.zeros((slabs, width), F32)
    for k, piece in enumerate(around(exchange_rows, ("x",), 1)):
        projected += jnp.dot(rows[k], piece, preferred_element_type=F32)
    return swapped(projected.astype(BF16).reshape(slabs, 2, -1), SLABS).reshape(1, CELLS)


def solution(mesh):
    split_mesh = Mesh(mesh.devices.reshape(4, 4, 2, 2, 8), AXES)
    placed = P(AXES, None)
    return jax.shard_map(steps, mesh=split_mesh, in_specs=placed, out_specs=placed, check_vma=False)
```

```python
import math
import numpy as np
import jax
import jax.numpy as jnp
from jax import lax
from jax.experimental import pallas as pl
from jax.experimental.pallas import tpu as pltpu
from jax.sharding import Mesh
from jax.sharding import PartitionSpec as P


GRID = 40
CELLS = GRID**3
F32 = jnp.float32
BF16 = jnp.bfloat16


def cosine_sums(values, size):
    half = size // 2
    out = [None] * (half + 1)
    if size % 4 == 0:
        mid = half // 2
        folded = [values[x] + values[half - x] for x in range(mid)] + [values[mid]]
        for b, term in enumerate(cosine_sums(folded, half)):
            out[2 * b] = term
        rest = [values[x] - values[half - x] for x in range(mid)]
        for a in range(1, half + 1, 2):
            out[a] = weighted(rest, [math.cos(2 * math.pi * (a * x % size) / size) for x in range(mid)])
    else:
        for a in range(half + 1):
            out[a] = weighted(values, [math.cos(2 * math.pi * (a * x % size) / size) for x in range(half + 1)])
    return out


def sine_sums(values, size):
    half = size // 2
    out = [None] * (half + 1)
    if size % 4 == 0:
        mid = half // 2
        folded = [None] + [values[x] - values[half - x] for x in range(1, mid)]
        for b, term in enumerate(sine_sums(folded, half)):
            if term is not None:
                out[2 * b] = term
        rest = [values[x] + values[half - x] for x in range(1, mid)] + [values[mid]]
        for a in range(1, half, 2):
            out[a] = weighted(rest, [math.sin(2 * math.pi * (a * x % size) / size) for x in range(1, mid + 1)])
    else:
        for a in range(1, half):
            out[a] = weighted(values[1:half], [math.sin(2 * math.pi * (a * x % size) / size) for x in range(1, half)])
    return out


def weighted(values, weights):
    groups = {}
    for value, weight in zip(values, weights, strict=True):
        size = round(abs(weight), 12)
        if size == 0.0:
            continue
        groups.setdefault(size, []).append(value if weight > 0 else (value,))
    total = None
    for size, members in groups.items():
        part = None
        for m in members:
            if isinstance(m, tuple):
                part = -m[0] if part is None else part - m[0]
            else:
                part = m if part is None else part + m
        part = part if size == 1.0 else part * size
        total = part if total is None else total + part
    return total


def hartley(values):
    size = len(values)
    half = size // 2
    even = [values[0]] + [values[x] + values[size - x] for x in range(1, half)] + [values[half]]
    odd = [None] + [values[x] - values[size - x] for x in range(1, half)]
    cosines, sines = cosine_sums(even, size), sine_sums(odd, size)
    out = [None] * size
    out[0], out[half] = cosines[0], cosines[half]
    for a in range(1, half):
        out[a] = cosines[a] + sines[a]
        out[size - a] = cosines[a] - sines[a]
    return out


def split(x):
    high = x.astype(BF16)
    return high, (x - high.astype(F32)).astype(BF16)


def along_lanes(x, table_high, table_low):
    high, low = split(x)
    out = jnp.dot(high, table_high, preferred_element_type=F32)
    out += jnp.dot(low, table_high, preferred_element_type=F32)
    return out + jnp.dot(high, table_low, preferred_element_type=F32)


ROWS = 200


def exchange_kernel(o_ref, a_ref, b_ref, table_ref, kernel_ref, out_ref, field, sources):
    high, low = table_ref[0], table_ref[1]

    @pl.loop(0, GRID * GRID // ROWS)
    def _(step):
        rows = pl.ds(pl.multiple_of(step * ROWS, 8), ROWS)
        o = o_ref[rows, :].astype(F32)
        three = jnp.concatenate(
            [o, a_ref[rows, :].astype(F32), b_ref[rows, :].astype(F32), jnp.zeros((ROWS, 8), F32)], axis=1
        )
        target = jnp.concatenate([o, o, o, jnp.zeros((ROWS, 8), F32)], axis=1)
        sources[rows, :] = three
        field[rows, :] = along_lanes(target * three, high, low)

    @pl.loop(0, GRID // 8)
    def _(chunk):
        rows = [pl.ds(pl.multiple_of(GRID * x + 8 * chunk, 8), 8) for x in range(GRID)]
        for x, value in enumerate(hartley([field[r, :] for r in rows])):
            field[rows[x], :] = value

    @pl.loop(0, GRID // 8)
    def _(chunk):
        rows = [pl.ds(y + GRID * 8 * chunk, 8, stride=GRID) for y in range(GRID)]
        spectrum = hartley([field[r, :] for r in rows])
        around = pl.ds(pl.multiple_of(8 * chunk, 8), 8)
        spectrum = [v * kernel_ref[min(b, GRID - b), around, :] for b, v in enumerate(spectrum)]
        for y, value in enumerate(hartley(spectrum)):
            field[rows[y], :] = value

    @pl.loop(0, GRID // 8)
    def _(chunk):
        rows = [pl.ds(pl.multiple_of(GRID * x + 8 * chunk, 8), 8) for x in range(GRID)]
        for x, value in enumerate(hartley([field[r, :] for r in rows])):
            field[rows[x], :] = value

    @pl.loop(0, GRID * GRID // ROWS)
    def _(step):
        rows = pl.ds(pl.multiple_of(step * ROWS, 8), ROWS)
        terms = sources[rows, :] * along_lanes(field[rows, :], high, low)
        total = terms + pltpu.roll(terms, 128 - GRID, axis=1) + pltpu.roll(terms, 128 - 2 * GRID, axis=1)
        out_ref[rows, :] = (-total[:, :GRID]).astype(BF16)


def hartley_tables():
    index = np.arange(GRID)
    angle = 2 * np.pi / GRID * (index[:, None] * index[None, :] % GRID)
    cas = (np.cos(angle) + np.sin(angle)).astype(np.float32)
    table = np.zeros((128, 128), np.float32)
    for s in range(3):
        table[GRID * s : GRID * (s + 1), GRID * s : GRID * (s + 1)] = cas
    high = jnp.asarray(table).astype(BF16)
    low = (jnp.asarray(table) - high.astype(F32)).astype(BF16)
    return jnp.stack([high, low])


def kernel_table():
    freq = np.arange(GRID)
    wave = 2 * np.pi / GRID * np.where(freq <= GRID // 2, freq, freq - GRID)
    square = wave * wave
    total = square[: GRID // 2 + 1, None, None] + square[None, :, None] + square[None, None, :]
    safe = np.where(total > 0, total, 1.0)
    table = np.where(total > 0, 4 * (1 - np.exp(-0.25 * total)) / safe, 1.0) / CELLS
    out = np.zeros((GRID // 2 + 1, GRID, 128), np.float32)
    for s in range(3):
        out[:, :, GRID * s : GRID * (s + 1)] = table
    return jnp.asarray(out)


def exchange_of(o, a, b):
    square = GRID * GRID
    return pl.pallas_call(
        exchange_kernel,
        out_shape=jax.ShapeDtypeStruct((square, GRID), BF16),
        in_specs=[pl.BlockSpec(memory_space=pltpu.VMEM)] * 5,
        out_specs=pl.BlockSpec(memory_space=pltpu.VMEM),
        scratch_shapes=[pltpu.VMEM((square, 128), F32), pltpu.VMEM((square, 128), F32)],
        compiler_params=pltpu.CompilerParams(vmem_limit_bytes=32 << 20),
        cost_estimate=pl.CostEstimate(flops=10_000_000, bytes_accessed=4_000_000, transcendentals=0),
        name="exchange",
    )(o.reshape(square, GRID), a.reshape(square, GRID), b.reshape(square, GRID), hartley_tables(), kernel_table())


N = 512
BLOCK = 128


def thirds(x):
    high = x.astype(BF16)
    rest = x - high.astype(F32)
    middle = rest.astype(BF16)
    return high, middle, (rest - middle.astype(F32)).astype(BF16)


def exact_dot(a, b):
    (a0, a1, a2), (b0, b1, b2) = a, b
    top = jnp.concatenate([b0, b1], axis=0)
    d = lambda p, q, r: jnp.dot(jnp.concatenate([p, q], axis=1), r, preferred_element_type=F32)
    return d(a0, a0, top) + (d(a1, a1, top) + d(a0, a2, jnp.concatenate([b2, b0], axis=0)))


def exact_dot_t(a, b):
    (a0, a1, a2), (b0, b1, b2) = thirds(a), thirds(b)
    d = lambda p, q: lax.dot_general(p, q, (((1,), (1,)), ((), ())), preferred_element_type=F32)
    return d(a0, b0) + (d(a0, b1) + d(a1, b0)) + (d(a1, b1) + d(a0, b2) + d(a2, b0))


def invert_block(groups):
    sub = lax.broadcasted_iota(jnp.int32, (8, BLOCK), 0)
    lane = lax.broadcasted_iota(jnp.int32, (8, BLOCK), 1)
    wide = lambda x, j: jnp.broadcast_to(x[j : j + 1, :], (8, BLOCK))
    size = 16
    count = size // 8
    pair = range(count)
    for p in range(BLOCK // size):
        first = size * p
        here = (lane >= first) & (lane < first + size)
        column = lambda v, k: jnp.broadcast_to(groups[v][:, first + k : first + k + 1], (8, BLOCK))
        pivots = [[column(count * p + g, k) for g in pair] for k in range(size)]
        panel = [
            jnp.where(here, jnp.where(lane - first - 8 * g == sub, 1.0, 0.0), groups[count * p + g]) for g in pair
        ]
        lower = [jnp.zeros((8, BLOCK), F32) for _ in pair]
        scale = [jnp.zeros((8, BLOCK), F32) for _ in pair]
        for j in range(size):
            gj, sj = j // 8, j % 8
            r = 1.0 / wide(pivots[j][gj], sj)
            factor = [(jnp.where(sub == sj, 0.0, pivots[j][g]) if g == gj else pivots[j][g]) * r for g in pair]
            row = wide(panel[gj], sj)
            lower[gj] = jnp.where(sub == sj, row, lower[gj])
            scale[gj] = jnp.where(sub == sj, r, scale[gj])
            for k in range(j + 1, size):
                across = wide(pivots[k][gj], sj)
                pivots[k] = [pivots[k][g] - factor[g] * across for g in pair]
            panel = [panel[g] - factor[g] * row for g in pair]
        panel = [panel[g] * scale[g] for g in pair]
        for g in pair:
            groups[count * p + g] = lower[g] * jnp.sqrt(scale[g])
        spread = [wide(panel[k // 8], k % 8) for k in range(size)]
        for v in range(count * (p + 1), BLOCK // 8):
            parts = [column(v, k) * spread[k] for k in range(size)]
            while len(parts) > 1:
                parts = [a + b for a, b in zip(parts[::2], parts[1::2])]
            value = jnp.where(here, 0.0, groups[v]) - parts[0]
            groups[v] = value
    return groups


def factor_kernel(place_ref, parts_ref, out_ref, m, w, x):
    core, shelf, column, block = place_ref[0], place_ref[1], place_ref[2], place_ref[3]
    for r in range(4):
        for q in range(4):
            for p in range(4):
                top = BLOCK * p + 32 * q
                m[top : top + 32, BLOCK * r : BLOCK * (r + 1)] = parts_ref[
                    (p // 2) ^ core, 4 * r + q, 32 * (p % 2) : 32 * (p % 2) + 32, :
                ]
    rows = lambda i: slice(BLOCK * i, BLOCK * (i + 1))
    eye = lax.broadcasted_iota(jnp.int32, (BLOCK, BLOCK), 0) == lax.broadcasted_iota(jnp.int32, (BLOCK, BLOCK), 1)
    sums = [jnp.zeros((1, BLOCK), F32) for _ in range(4)]
    trace = jnp.zeros((1, BLOCK), F32)
    for i in range(4):
        for j in range(i + 1):
            s = (m[rows(i), rows(j)] + m[rows(j), rows(i)].T) * (-0.5 / CELLS)
            sums[j] = sums[j] + jnp.sum(jnp.abs(s), axis=0, keepdims=True)
            if i != j:
                flipped = s.T
                m[rows(j), rows(i)] = flipped
                sums[i] = sums[i] + jnp.sum(jnp.abs(flipped), axis=0, keepdims=True)
            else:
                m[rows(i), rows(i)] = s
                trace = trace + jnp.sum(jnp.where(eye, jnp.abs(s), 0.0), axis=0, keepdims=True)
    gamma = jnp.sum(trace, axis=1, keepdims=True) / N + 1e-6
    for i in range(4):
        m[rows(i), rows(i)] = m[rows(i), rows(i)] + jnp.where(eye, sums[i] + gamma, 0.0)
    keep = lax.broadcasted_iota(jnp.int32, (BLOCK, BLOCK), 0) >= lax.broadcasted_iota(jnp.int32, (BLOCK, BLOCK), 1)

    @pl.loop(0, 4)
    def _(step):
        here = pl.ds(pl.multiple_of(step * BLOCK, BLOCK), BLOCK)
        groups = [m[pl.ds(pl.multiple_of(step * BLOCK + 8 * v, 8), 8), here] for v in range(BLOCK // 8)]
        for v, value in enumerate(invert_block(groups)):
            w[8 * v : 8 * v + 8, :] = value
        m[here, here] = jnp.where(keep, w[...], 0.0)
        for s in range(3):

            @pl.when(step == s)
            def _():
                start = BLOCK * (s + 1)
                right = exact_dot(thirds(m[rows(s), rows(s)]), thirds(m[rows(s), start:]))
                m[rows(s), start:] = right
                pieces = thirds(right)
                for i in range(s + 1, 4):
                    begin = BLOCK * (i - s - 1)
                    left = thirds(right[:, begin : begin + BLOCK].T)
                    m[rows(i), BLOCK * i :] = m[rows(i), BLOCK * i :] - exact_dot(left, [t[:, begin:] for t in pieces])

    x[...] = jnp.zeros_like(x)
    mine = pl.ds(pl.multiple_of(32 * block, 32), 32)
    own = pl.ds(pl.multiple_of(BLOCK * shelf, BLOCK), BLOCK)
    x[:, own] = m[mine, own]
    for j in (2, 1, 0):

        @pl.when(j < shelf)
        def _():
            start = BLOCK * (j + 1)
            total = exact_dot_t(x[:, start:], m[rows(j), start:])
            x[:, rows(j)] = -exact_dot(thirds(total), thirds(m[rows(j), rows(j)]))

    lane = lax.broadcasted_iota(jnp.int32, (32, BLOCK), 1)
    for k in range(4):
        s = lax.rem(column + 4 - k, 4)
        total = jnp.zeros((32, BLOCK), F32)
        for p in range(4):
            turned = pltpu.roll(x[:, rows(p)], lax.rem(p + 4 - s, 4) * 32, axis=1)
            total = jnp.where(lane // 32 == p, turned, total)
        out_ref[k] = total.astype(BF16)


def inverse_rows(place, parts):
    return pl.pallas_call(
        factor_kernel,
        out_shape=jax.ShapeDtypeStruct((4, 32, BLOCK), BF16),
        in_specs=[pl.BlockSpec(memory_space=pltpu.SMEM), pl.BlockSpec(memory_space=pltpu.VMEM)],
        out_specs=pl.BlockSpec(memory_space=pltpu.VMEM),
        scratch_shapes=[pltpu.VMEM((N, N), F32), pltpu.VMEM((BLOCK, BLOCK), F32), pltpu.VMEM((32, N), F32)],
        compiler_params=pltpu.CompilerParams(vmem_limit_bytes=32 << 20),
        cost_estimate=pl.CostEstimate(flops=400_000_000, bytes_accessed=4_000_000, transcendentals=0),
        name="factor",
    )(place, parts)


AXES = ("yh", "x", "c", "yl", "z")
BLOCKS = ("yh", "x", "c")
SLABS = ("c", "yl", "z")
QUARTER = ("c", "yl")
PLANE = ("yh", "x", "yl")


def shifted(value, axes, steps):
    count = lax.axis_size(axes)
    return lax.ppermute(value, axes, [(i, (i + steps) % count) for i in range(count)])


def swapped(tiles, axes):
    return lax.all_to_all(tiles, axes, split_axis=0, concat_axis=0, tiled=True)


def shown_to(value, axes):
    return swapped(jnp.broadcast_to(value, (lax.axis_size(axes), *value.shape)), axes)


def gathered_slab(row, axis, last):
    slabs, copies = lax.axis_size(SLABS), lax.axis_size(axis)
    tiles = row.reshape(slabs, 2, -1)
    if last:
        tiles = jnp.broadcast_to(tiles[:, None], (slabs, copies, *tiles.shape[1:]))
        tiles = swapped(tiles.reshape(slabs * copies, *tiles.shape[2:]), (*SLABS, axis))
        tiles = jnp.swapaxes(tiles.reshape(slabs, copies, *tiles.shape[1:]), 0, 1)
    else:
        tiles = jnp.broadcast_to(tiles[None], (copies, *tiles.shape))
        tiles = swapped(tiles.reshape(copies * slabs, *tiles.shape[2:]), (axis, *SLABS))
    return tiles.reshape(copies * slabs, -1)


def around(value, axes, way):
    pieces = [value]
    for k in range(1, lax.axis_size(axes)):
        pieces.append(shifted(value, axes, way * k))
    return pieces


def steps(orbitals):
    slabs = lax.axis_size(SLABS)
    width = CELLS // slabs
    first, second = shifted(orbitals, BLOCKS, 1), shifted(orbitals, BLOCKS, 2)
    orbital_rows = gathered_slab(orbitals, "x", True)
    exchange = exchange_of(orbitals, first, second)
    exchange_rows = gathered_slab(exchange, "yh", False)
    margin = lax.dot_general(
        exchange_rows, orbital_rows, (((1,), (1,)), ((), ())), preferred_element_type=F32
    )
    summed = jnp.sum(swapped(margin.reshape(4, BLOCK // 4, BLOCK), QUARTER), axis=0)
    summed = jnp.sum(shown_to(summed, ("z",)), axis=0)
    mine = shown_to(summed, PLANE).reshape(16, BLOCK // 2, BLOCK)
    other = shifted(mine, ("c",), 1)
    place = jnp.stack([lax.axis_index(a) for a in ("c", "yh", "x", ("yh", "x"))]).astype(jnp.int32)
    rows = inverse_rows(place, jnp.stack([mine, other]))
    projected = jnp.zeros((slabs, width), F32)
    for k, piece in enumerate(around(exchange_rows, ("x",), 1)):
        projected += jnp.dot(rows[k], piece, preferred_element_type=F32)
    return swapped(projected.astype(BF16).reshape(slabs, 2, -1), SLABS).reshape(1, CELLS)


def solution(mesh):
    split_mesh = Mesh(mesh.devices.reshape(4, 4, 2, 2, 8), AXES)
    placed = P(AXES, None)
    return jax.shard_map(steps, mesh=split_mesh, in_specs=placed, out_specs=placed, check_vma=False)
```
